32 devices in a mesh: seq: 16 (over z, y, core), fsdp: 2 (over x).
Axes of the slice: x: 2, y: 2, z: 4, core: 2. Of those that a mesh axis runs over, the one named last changes fastest.
Arguments:
- tokens: float32 [2, 2048, 768], P('fsdp', 'seq'), may hold values from -36 to 36
- cotangent: float32 [2, 2048, 768], P('fsdp', 'seq'), may hold values from -6 to 6
- qkv_weight: bfloat16 [2, 768, 2304], P(None, ('seq', 'fsdp')), may hold values from -0.21875 to 0.21875
- out_weight: bfloat16 [2, 768, 768], P(None, ('seq', 'fsdp')), may hold values from -2.5 to 2.5
- up_weight: bfloat16 [2, 768, 2304], P(None, ('seq', 'fsdp')), may hold values from -0.21875 to 0.21875
- down_weight: bfloat16 [2, 768, 1152], P(None, ('seq', 'fsdp')), may hold values from -0.1875 to 0.1875
- attn_gain: bfloat16 [2, 768], P(None, ('seq', 'fsdp')), may hold values from 0.5 to 1.5
- mlp_gain: bfloat16 [2, 768], P(None, ('seq', 'fsdp')), may hold values from 0.5 to 1.5
Outputs:
- stream_out: float32 [2, 2048, 768], P('fsdp', 'seq')
- grad_tokens: float32 [2, 2048, 768], P('fsdp', 'seq')
- qkv_grad: float32 [2, 768, 2304], P(None, ('seq', 'fsdp'))
- out_grad: float32 [2, 768, 768], P(None, ('seq', 'fsdp'))
- up_grad: float32 [2, 768, 2304], P(None, ('seq', 'fsdp'))
- down_grad: float32 [2, 768, 1152], P(None, ('seq', 'fsdp'))
- attn_gain_grad: float32 [2, 768], P(None, ('seq', 'fsdp'))
- mlp_gain_grad: float32 [2, 768], P(None, ('seq', 'fsdp'))
The draws below stay inside these ranges and needn't reach their ends.
All inputs are finite; a program needn't handle non-finite values.
Results may differ from the reference program's by a relative error of at most 0.019.
Values may be sent and summed in bfloat16 or wider, within the bound.
No kernel may reach another device: no remote copies, remote signals or barrier semaphores. Data moves between devices by JAX's collectives and lax.ppermute only.
A program may use at most 256 MiB of HBM per device.

```python
import math
import jax
import jax.numpy as jnp
from jax import lax

D = 768
H = 12
HD = 64
FF = 1152
HALF = 64
LAYERS = 2
BLK = 128
SEQS = 2
LENGTH = 2048
TOKENS = 4096


def draw_tokens(key, part):
    row_key, col_key, noise_key = jax.random.split(key, 3)
    row_scale = jnp.exp(jax.random.uniform(row_key, (SEQS, LENGTH, 1), jnp.float32, math.log(0.3), math.log(3.0)))
    col_scale = jnp.exp(jax.random.uniform(col_key, (1, 1, D), jnp.float32, math.log(0.3), math.log(3.0)))
    noise_part = jnp.clip(jax.random.normal(noise_key, (SEQS, LENGTH, D), jnp.float32), -4.0, 4.0)
    return row_scale * col_scale * noise_part


def spiked(drawn, rng, source, target, blocks, factor):
    owner, partner = [(jnp.arange(drawn.shape[dim]) // (drawn.shape[dim] // blocks)).reshape([-1 if axis == dim else 1 for axis in range(drawn.ndim)]) for dim in (source, target)]
    chosen = jax.random.permutation(rng, blocks)[partner]
    strong = (owner == chosen) | (owner == (partner + blocks // 2) % blocks)
    return jnp.where(strong, factor * drawn, drawn)


def levels(key, dims, cuts, low, high):
    loudness, own = 1.0, jax.random.fold_in(key, 6)
    for axis_at, shards_of in cuts:
        steps = jnp.exp(jax.random.uniform(jax.random.fold_in(own, axis_at), (shards_of,), jnp.float32, low / len(cuts), high / len(cuts)))
        loudness = loudness * jnp.repeat(steps, dims[axis_at] // shards_of).reshape([-1 if axis == axis_at else 1 for axis in range(len(dims))])
    return loudness


def gaussian(own_key, extent, spread, bound, pieces=(), held_as=jnp.bfloat16):
    entries = jax.random.normal(own_key, extent, jnp.float32) * spread
    if len(pieces) > 0:
        entries = levels(own_key, extent, pieces, -0.22, 0.18) * entries
    return jnp.clip(entries, min=-bound, max=bound).astype(held_as)


def heavy_noise(stream_key, dims, deviation, reach, cuts, heavy, held_as=jnp.bfloat16):
    result = deviation * jax.random.normal(stream_key, dims, jnp.float32)
    if cuts:
        result = result * levels(stream_key, dims, cuts, -0.22, 0.18)
    return jnp.clip(spiked(result, jax.random.fold_in(stream_key, 3), *heavy), -reach, reach).astype(held_as)


def setup_inputs(seed: int = 0) -> dict:
    key_list = jax.random.split(jax.random.key(seed), 9)
    tokens = draw_tokens(jax.random.fold_in(key_list[8], 71), 0)
    cotangent = heavy_noise(key_list[1], (SEQS, LENGTH, D), 1.0, 6.0, ((0, 2), (1, 16)), (1, 2, 16, 2.0), jnp.float32)
    qkv_weight = gaussian(key_list[2], (LAYERS, D, 3 * D), D ** -0.5, 0.21875, ((1, 32),))
    out_weight = gaussian(key_list[3], (LAYERS, D, D), (D // (2 * HALF)) ** -0.5, 2.5, ((1, 32),))
    up_weight = gaussian(key_list[4], (LAYERS, D, 2 * FF), D ** -0.5, 0.21875, ((1, 32),))
    down_weight = gaussian(key_list[5], (LAYERS, D, FF), FF ** -0.5, 0.1875, ((1, 32),))
    attn_gain = jnp.clip(1.0 + 0.1 * jax.random.normal(key_list[6], (LAYERS, D), jnp.float32), 0.5, 1.5).astype(jnp.bfloat16)
    mlp_gain = jnp.clip(1.0 + 0.1 * jax.random.normal(key_list[7], (LAYERS, D), jnp.float32), 0.5, 1.5).astype(jnp.bfloat16)
    return dict(tokens=tokens, cotangent=cotangent, qkv_weight=qkv_weight, out_weight=out_weight, up_weight=up_weight, down_weight=down_weight, attn_gain=attn_gain, mlp_gain=mlp_gain)


norm_eps = 1e-05
rope_base = 10000.0
inv_root_two = 1.0 / math.sqrt(2.0)
inv_root_tau = 1.0 / math.sqrt(2.0 * math.pi)
highest = lax.Precision.HIGHEST

def layer_norm(values, norm_gain):
    center = values - lax.optimization_barrier(jnp.mean(values, axis=-1, keepdims=True))
    inv_scale = lax.rsqrt(lax.optimization_barrier(jnp.mean(center * center, axis=-1, keepdims=True)) + norm_eps)
    normed = center * inv_scale
    return (normed, inv_scale, normed * norm_gain.astype(jnp.float32))

def norm_back(grad_out, normed, inv_scale, norm_gain):
    grad_hat = grad_out * norm_gain.astype(jnp.float32)
    mean_one = lax.optimization_barrier(jnp.mean(grad_hat, axis=-1, keepdims=True))
    mean_two = lax.optimization_barrier(jnp.mean(grad_hat * normed, axis=-1, keepdims=True))
    return inv_scale * (grad_hat - mean_one - normed * mean_two)

def gelu_value(values):
    return 0.5 * values * (1.0 + lax.erf(values * inv_root_two))

def gelu_slope(values):
    return 0.5 * (1.0 + lax.erf(values * inv_root_two)) + values * inv_root_tau * jnp.exp(-0.5 * values * values)

def rope_tables(positions, head_size):
    frequency = rope_base ** (-jnp.arange(0, head_size, 2).astype(jnp.float32) / head_size)
    angles = positions[:, None] * frequency[None, :]
    cosine = jnp.cos(angles)
    sine_part = jnp.sin(angles)
    return (jnp.concatenate([cosine, cosine], axis=-1)[:, None, :], jnp.concatenate([sine_part, sine_part], axis=-1)[:, None, :])

def rotate_half(values):
    half_size = values.shape[-1] // 2
    return jnp.concatenate([-values[..., half_size:], values[..., :half_size]], axis=-1)

def rotate_back(values):
    half_size = values.shape[-1] // 2
    return jnp.concatenate([values[..., half_size:], -values[..., :half_size]], axis=-1)

def band_mask(query_count, halo_width, key_valid):
    query_pos = jnp.arange(query_count)[:, None]
    key_index = jnp.arange(query_count + 2 * halo_width)[None, :]
    offset = key_index - query_pos
    inside = (offset >= 0) & (offset <= 2 * halo_width)
    return inside[None, None, :, :] & key_valid[:, None, None, :]

def attend_forward(query_b, key_win, value_win, window_mask, score_scale):
    scores = jnp.einsum('bqhe,bkhe->bhqk', query_b.astype(jnp.float32), key_win.astype(jnp.float32), precision=highest) * score_scale
    scores = jnp.where(window_mask, scores, -jnp.inf)
    log_total = jnp.log(lax.optimization_barrier(jnp.sum(jnp.exp(scores), axis=-1)))
    probs_b = lax.optimization_barrier(jnp.exp(scores - log_total[..., None]).astype(jnp.bfloat16))
    attended = jnp.einsum('bhqk,bkhe->bqhe', probs_b.astype(jnp.float32), value_win.astype(jnp.float32), precision=highest)
    return (attended.astype(jnp.bfloat16), log_total)

def attend_backward(query_b, key_win, value_win, window_mask, log_total, grad_attended, score_scale):
    query_f = query_b.astype(jnp.float32)
    key_f = key_win.astype(jnp.float32)
    value_f = value_win.astype(jnp.float32)
    grad_f = grad_attended.astype(jnp.float32)
    scores = jnp.einsum('bqhe,bkhe->bhqk', query_f, key_f, precision=highest) * score_scale
    scores = jnp.where(window_mask, scores, -jnp.inf)
    attn_probs = jnp.exp(scores - log_total[..., None])
    probs_b = lax.optimization_barrier(attn_probs.astype(jnp.bfloat16))
    grad_value = jnp.einsum('bhqk,bqhe->bkhe', probs_b.astype(jnp.float32), grad_f, precision=highest)
    grad_probs = jnp.einsum('bqhe,bkhe->bhqk', grad_f, value_f, precision=highest)
    row_inner = lax.optimization_barrier(jnp.sum(attn_probs * grad_probs, axis=-1, keepdims=True))
    grad_scores = lax.optimization_barrier((attn_probs * (grad_probs - row_inner) * score_scale).astype(jnp.bfloat16))
    scores_f = grad_scores.astype(jnp.float32)
    grad_query = jnp.einsum('bhqk,bkhe->bqhe', scores_f, key_f, precision=highest)
    grad_key = jnp.einsum('bhqk,bqhe->bkhe', scores_f, query_f, precision=highest)
    return (grad_query, grad_key, grad_value)

def windows(values, block_size):
    block_count = values.shape[0] // block_size
    blocks = values.reshape((block_count, block_size) + values.shape[1:])
    zero_edge = jnp.zeros((1, HALF) + values.shape[1:], values.dtype)
    left_part = jnp.concatenate([zero_edge, blocks[:-1, block_size - HALF:]], axis=0)
    right_part = jnp.concatenate([blocks[1:, :HALF], zero_edge], axis=0)
    return jnp.concatenate([left_part, blocks, right_part], axis=1)

def fold_windows(window_grads, block_size):
    block_count = window_grads.shape[0]
    center = window_grads[:, HALF:HALF + block_size]
    zero_edge = jnp.zeros((1, HALF) + window_grads.shape[2:], window_grads.dtype)
    head_part = jnp.concatenate([zero_edge, window_grads[:-1, HALF + block_size:]], axis=0)
    tail_part = jnp.concatenate([window_grads[1:, :HALF], zero_edge], axis=0)
    middle = jnp.zeros((block_count, block_size - 2 * HALF) + window_grads.shape[2:], window_grads.dtype)
    total = center + jnp.concatenate([head_part, middle, tail_part], axis=1)
    return total.reshape((block_count * block_size,) + window_grads.shape[2:])

def reference(tokens, cotangent, qkv_weight, out_weight, up_weight, down_weight, attn_gain, mlp_gain):
    block_count = LENGTH // BLK
    width_keys = BLK + 2 * HALF
    score_scale = 1.0 / math.sqrt(HD)
    positions = jnp.arange(LENGTH).astype(jnp.float32)
    cosine_table, sine_table = rope_tables(positions, HD)
    key_pos = (jnp.arange(block_count) * BLK)[:, None] - HALF + jnp.arange(width_keys)[None, :]
    key_valid = (key_pos >= 0) & (key_pos < LENGTH)
    window_mask = band_mask(BLK, HALF, key_valid)

    def forward_block(operands):
        query_blk, key_blk, value_blk, mask_blk = operands
        attended, log_total = attend_forward(query_blk[None], key_blk[None], value_blk[None], mask_blk[None], score_scale)
        return (attended[0], log_total[0])

    def backward_block(operands):
        query_blk, key_blk, value_blk, mask_blk, total_blk, grad_blk = operands
        grad_query, grad_key, grad_value = attend_backward(query_blk[None], key_blk[None], value_blk[None], mask_blk[None], total_blk[None], grad_blk[None], score_scale)
        return (grad_query[0], grad_key[0], grad_value[0])

    def sequence_pass(grad_sums, operands):
        stream, grad_stream = operands
        layer_store = []
        for layer_index in range(LAYERS):
            normed_one, scale_one, pre_one = layer_norm(stream, attn_gain[layer_index])
            attn_in = pre_one.astype(jnp.bfloat16)
            projected = jnp.dot(attn_in, qkv_weight[layer_index], preferred_element_type=jnp.float32)
            query_raw = projected[:, :D].reshape(LENGTH, H, HD)
            key_raw = projected[:, D:2 * D].reshape(LENGTH, H, HD)
            query_b = (query_raw * cosine_table + rotate_half(query_raw) * sine_table).astype(jnp.bfloat16)
            key_b = (key_raw * cosine_table + rotate_half(key_raw) * sine_table).astype(jnp.bfloat16)
            value_b = projected[:, 2 * D:].reshape(LENGTH, H, HD).astype(jnp.bfloat16)
            query_blocks = query_b.reshape(block_count, BLK, H, HD)
            key_win = windows(key_b, BLK)
            value_win = windows(value_b, BLK)
            attended, log_total = lax.map(forward_block, (query_blocks, key_win, value_win, window_mask))
            attended = attended.reshape(LENGTH, D)
            middle = stream + jnp.dot(attended, out_weight[layer_index], preferred_element_type=jnp.float32)
            normed_two, scale_two, pre_two = layer_norm(middle, mlp_gain[layer_index])
            ffn_in = pre_two.astype(jnp.bfloat16)
            lifted = jnp.dot(ffn_in, up_weight[layer_index], preferred_element_type=jnp.float32)
            gate_part = lifted[:, :FF]
            linear_part = lifted[:, FF:]
            hidden_b = (gelu_value(gate_part) * linear_part).astype(jnp.bfloat16)
            layer_store.append((normed_one, scale_one, attn_in, query_blocks, key_win, value_win, log_total, attended, normed_two, scale_two, ffn_in, gate_part, linear_part, hidden_b))
            stream = middle + jnp.dot(hidden_b, down_weight[layer_index].T, preferred_element_type=jnp.float32)
        sums = list(grad_sums)
        for layer_index in reversed(range(LAYERS)):
            normed_one, scale_one, attn_in, query_blocks, key_win, value_win, log_total, attended, normed_two, scale_two, ffn_in, gate_part, linear_part, hidden_b = layer_store[layer_index]
            grad_b = grad_stream.astype(jnp.bfloat16)
            down_sum = jnp.dot(grad_b.T, hidden_b, preferred_element_type=jnp.float32)
            grad_hidden = jnp.dot(grad_b, down_weight[layer_index], preferred_element_type=jnp.float32)
            grad_lifted = jnp.concatenate([grad_hidden * linear_part * gelu_slope(gate_part), grad_hidden * gelu_value(gate_part)], axis=1).astype(jnp.bfloat16)
            up_sum = jnp.dot(ffn_in.T, grad_lifted, preferred_element_type=jnp.float32)
            grad_ffn_in = jnp.dot(grad_lifted, up_weight[layer_index].T, preferred_element_type=jnp.float32)
            gain_two_sum = lax.optimization_barrier(jnp.sum(grad_ffn_in * normed_two, axis=0))
            grad_middle = grad_stream + norm_back(grad_ffn_in, normed_two, scale_two, mlp_gain[layer_index])
            grad_middle_b = grad_middle.astype(jnp.bfloat16)
            out_sum = jnp.dot(attended.T, grad_middle_b, preferred_element_type=jnp.float32)
            grad_attended = jnp.dot(grad_middle_b, out_weight[layer_index].T, preferred_element_type=jnp.float32).astype(jnp.bfloat16)
            grad_attended = grad_attended.reshape(block_count, BLK, H, HD)
            grad_query, grad_key_win, grad_value_win = lax.map(backward_block, (query_blocks, key_win, value_win, window_mask, log_total, grad_attended))
            grad_query = grad_query.reshape(LENGTH, H, HD)
            grad_key = fold_windows(grad_key_win, BLK)
            grad_value = fold_windows(grad_value_win, BLK)
            grad_query_pre = grad_query * cosine_table + rotate_back(grad_query * sine_table)
            grad_key_pre = grad_key * cosine_table + rotate_back(grad_key * sine_table)
            grad_projected = jnp.concatenate([grad_query_pre.reshape(LENGTH, D), grad_key_pre.reshape(LENGTH, D), grad_value.reshape(LENGTH, D)], axis=1).astype(jnp.bfloat16)
            qkv_sum = jnp.dot(attn_in.T, grad_projected, preferred_element_type=jnp.float32)
            grad_attn_in = jnp.dot(grad_projected, qkv_weight[layer_index].T, preferred_element_type=jnp.float32)
            gain_one_sum = lax.optimization_barrier(jnp.sum(grad_attn_in * normed_one, axis=0))
            grad_stream = grad_middle + norm_back(grad_attn_in, normed_one, scale_one, attn_gain[layer_index])
            sums[0] = sums[0].at[layer_index].add(qkv_sum)
            sums[1] = sums[1].at[layer_index].add(out_sum)
            sums[2] = sums[2].at[layer_index].add(up_sum)
            sums[3] = sums[3].at[layer_index].add(down_sum)
            sums[4] = sums[4].at[layer_index].add(gain_one_sum)
            sums[5] = sums[5].at[layer_index].add(gain_two_sum)
        return (tuple(sums), (stream, grad_stream))
    zero_sums = (jnp.zeros((LAYERS, D, 3 * D), jnp.float32), jnp.zeros((LAYERS, D, D), jnp.float32), jnp.zeros((LAYERS, D, 2 * FF), jnp.float32), jnp.zeros((LAYERS, D, FF), jnp.float32), jnp.zeros((LAYERS, D), jnp.float32), jnp.zeros((LAYERS, D), jnp.float32))
    grad_sums, (stream_out, grad_tokens) = lax.scan(sequence_pass, zero_sums, (tokens, cotangent))
    grad_factor = 1.0 / math.sqrt(TOKENS)
    return (stream_out, grad_tokens, grad_sums[0] * grad_factor, grad_sums[1] * grad_factor, grad_sums[2] * grad_factor, grad_sums[3] * grad_factor, grad_sums[4] * grad_factor, grad_sums[5] * grad_factor)
```

```python
import math

import jax
import jax.numpy as jnp
from jax import lax
from jax.sharding import PartitionSpec as P

D = 768
H = 12
HD = 64
FF = 1152
HALF = 64
LAYERS = 2
LANES = 128


norm_eps = 1e-05
rope_base = 10000.0
inv_root_two = 1.0 / math.sqrt(2.0)
inv_root_tau = 1.0 / math.sqrt(2.0 * math.pi)


def with_halo(cells, sides, width):
    for axis, dim in sides:
        count = lax.axis_size(axis)
        ends = count - 1
        head = lax.slice_in_dim(cells, 0, width, axis=dim)
        tail = lax.slice_in_dim(cells, cells.shape[dim] - width, cells.shape[dim], axis=dim)
        cells = jnp.concatenate(
            [
                lax.ppermute(tail, axis, [(i, (i + 1) % count) for i in range(ends)]),
                cells,
                lax.ppermute(head, axis, [((i + 1) % count, i) for i in range(ends)]),
            ],
            axis=dim,
        )
    return cells


def layer_norm(values, norm_gain):
    center = values - jnp.mean(values, axis=-1, keepdims=True)
    inv_scale = lax.rsqrt(jnp.mean(center * center, axis=-1, keepdims=True) + norm_eps)
    normed = center * inv_scale
    return (normed, inv_scale, normed * norm_gain.astype(jnp.float32))


def norm_back(grad_out, normed, inv_scale, norm_gain):
    grad_hat = grad_out * norm_gain.astype(jnp.float32)
    mean_one = jnp.mean(grad_hat, axis=-1, keepdims=True)
    mean_two = jnp.mean(grad_hat * normed, axis=-1, keepdims=True)
    return inv_scale * (grad_hat - mean_one - normed * mean_two)


def gelu_value(values):
    return 0.5 * values * (1.0 + lax.erf(values * inv_root_two))


def gelu_slope(values):
    return 0.5 * (1.0 + lax.erf(values * inv_root_two)) + values * inv_root_tau * jnp.exp(
        -0.5 * values * values
    )


def rope_tables(positions, head_size):
    frequency = rope_base ** (-jnp.arange(0, head_size, 2).astype(jnp.float32) / head_size)
    angles = positions[:, None] * frequency[None, :]
    cosine = jnp.cos(angles)
    sine_part = jnp.sin(angles)
    return (
        jnp.concatenate([cosine, cosine], axis=-1)[:, None, :],
        jnp.concatenate([sine_part, sine_part], axis=-1)[:, None, :],
    )


def rotate_half(values):
    half_size = values.shape[-1] // 2
    return jnp.concatenate([-values[..., half_size:], values[..., :half_size]], axis=-1)


def rotate_back(values):
    half_size = values.shape[-1] // 2
    return jnp.concatenate([values[..., half_size:], -values[..., :half_size]], axis=-1)


def band_mask(query_count, halo_width, key_valid):
    query_pos = jnp.arange(query_count)[:, None]
    key_index = jnp.arange(query_count + 2 * halo_width)[None, :]
    offset = key_index - query_pos
    inside = (offset >= 0) & (offset <= 2 * halo_width)
    return inside[None, None, :, :] & key_valid[:, None, None, :]


def dot_rows(left_side, right_side):
    return lax.dot_general(
        left_side, right_side, (((0,), (0,)), ((), ())), preferred_element_type=jnp.float32
    )


def dot_cols(left_side, right_side):
    return lax.dot_general(
        left_side, right_side, (((1,), (1,)), ((), ())), preferred_element_type=jnp.float32
    )


def attend_forward(query_b, key_win, value_win, window_mask, score_scale):
    scores = (
        jnp.einsum("bqhe,bkhe->bhqk", query_b, key_win, preferred_element_type=jnp.float32)
        * score_scale
    )
    scores = jnp.where(window_mask, scores, -jnp.inf)
    log_total = jnp.log(jnp.sum(jnp.exp(scores), axis=-1))
    probs_b = jnp.exp(scores - log_total[..., None]).astype(jnp.bfloat16)
    attended = jnp.einsum("bhqk,bkhe->bqhe", probs_b, value_win, preferred_element_type=jnp.float32)
    return (attended.astype(jnp.bfloat16), log_total)


def attend_backward(
    query_b, key_win, value_win, window_mask, log_total, grad_attended, score_scale
):
    scores = (
        jnp.einsum("bqhe,bkhe->bhqk", query_b, key_win, preferred_element_type=jnp.float32)
        * score_scale
    )
    scores = jnp.where(window_mask, scores, -jnp.inf)
    attn_probs = jnp.exp(scores - log_total[..., None])
    probs_b = attn_probs.astype(jnp.bfloat16)
    grad_value = jnp.einsum(
        "bhqk,bqhe->bkhe", probs_b, grad_attended, preferred_element_type=jnp.float32
    )
    grad_probs = jnp.einsum(
        "bqhe,bkhe->bhqk", grad_attended, value_win, preferred_element_type=jnp.float32
    )
    row_inner = jnp.sum(attn_probs * grad_probs, axis=-1, keepdims=True)
    grad_scores = (attn_probs * (grad_probs - row_inner) * score_scale).astype(jnp.bfloat16)
    grad_query = jnp.einsum(
        "bhqk,bkhe->bqhe", grad_scores, key_win, preferred_element_type=jnp.float32
    )
    grad_key = jnp.einsum(
        "bhqk,bqhe->bkhe", grad_scores, query_b, preferred_element_type=jnp.float32
    )
    return (grad_query, grad_key, grad_value)


def gather_layer(qkv, out, up, down, gain_one, gain_two):
    rows = qkv.shape[0]
    gains = jnp.pad(jnp.stack([gain_one, gain_two], axis=1), ((0, 0), (0, LANES - 2)))
    packed = jnp.concatenate([qkv, out, up, down, gains], axis=1)
    whole = lax.all_gather(packed, ("seq", "fsdp"), axis=0, tiled=True)
    first = 0
    parts = []
    for width in (qkv.shape[1], out.shape[1], up.shape[1], down.shape[1], LANES):
        parts.append(whole[:, first : first + width])
        first += width
    return (parts[4][:, 0], parts[0], parts[1], parts[4][:, 1], parts[2], parts[3])


def scatter_layer(blocks, gain_vecs, grad_factor):
    gains = jnp.pad(jnp.stack(gain_vecs, axis=1), ((0, 0), (0, LANES - 2)))
    packed = jnp.concatenate(
        [part.astype(jnp.bfloat16) for part in (*blocks, gains)], axis=1
    )
    own = lax.psum_scatter(packed, ("seq", "fsdp"), scatter_dimension=0, tiled=True)
    own = own.astype(jnp.float32) * grad_factor
    first = 0
    parts = []
    for part in blocks:
        parts.append(own[:, first : first + part.shape[1]])
        first += part.shape[1]
    return (*parts, own[:, first], own[:, first + 1])


def local(tokens, cotangent, qkv_weight, out_weight, up_weight, down_weight, attn_gain, mlp_gain):
    row_count = tokens.shape[1]
    seq_count = lax.axis_size("seq")
    shard_count = lax.axis_size("fsdp")
    first_row = lax.axis_index("seq") * row_count
    length = row_count * seq_count
    width_keys = row_count + 2 * HALF
    score_scale = 1.0 / math.sqrt(HD)
    grad_factor = 1.0 / math.sqrt(length * shard_count)
    positions = (first_row + jnp.arange(row_count)).astype(jnp.float32)
    cosine_table, sine_table = rope_tables(positions, HD)
    key_pos = first_row - HALF + jnp.arange(width_keys)
    key_valid = ((key_pos >= 0) & (key_pos < length))[None, :]
    window_mask = band_mask(row_count, HALF, key_valid)
    stream = tokens.reshape(row_count, D)
    gains_one, qkv_all, out_all, gains_two, up_all, down_all = zip(
        *(
            gather_layer(
                qkv_weight[n], out_weight[n], up_weight[n], down_weight[n], attn_gain[n], mlp_gain[n]
            )
            for n in range(LAYERS)
        )
    )
    layer_store = []
    for layer_index in range(LAYERS):
        normed_one, scale_one, pre_one = layer_norm(stream, gains_one[layer_index])
        attn_in = pre_one.astype(jnp.bfloat16)
        projected = jnp.dot(attn_in, qkv_all[layer_index], preferred_element_type=jnp.float32)
        query_raw = projected[:, :D].reshape(row_count, H, HD)
        key_raw = projected[:, D : 2 * D].reshape(row_count, H, HD)
        query_b = (query_raw * cosine_table + rotate_half(query_raw) * sine_table).astype(
            jnp.bfloat16
        )
        key_b = (key_raw * cosine_table + rotate_half(key_raw) * sine_table).astype(jnp.bfloat16)
        value_b = projected[:, 2 * D :].astype(jnp.bfloat16)
        key_value = jnp.concatenate([key_b.reshape(row_count, D), value_b], axis=1)[None]
        padded = with_halo(key_value, (("seq", 1),), HALF)
        key_win = padded[:, :, :D].reshape(1, width_keys, H, HD)
        value_win = padded[:, :, D:].reshape(1, width_keys, H, HD)
        query_b = query_b.reshape(1, row_count, H, HD)
        attended, log_total = attend_forward(query_b, key_win, value_win, window_mask, score_scale)
        attended = attended.reshape(row_count, D)
        middle = stream + jnp.dot(
            attended, out_all[layer_index], preferred_element_type=jnp.float32
        )
        normed_two, scale_two, pre_two = layer_norm(middle, gains_two[layer_index])
        ffn_in = pre_two.astype(jnp.bfloat16)
        lifted = jnp.dot(ffn_in, up_all[layer_index], preferred_element_type=jnp.float32)
        gate_part = lifted[:, :FF]
        linear_part = lifted[:, FF:]
        hidden_b = (gelu_value(gate_part) * linear_part).astype(jnp.bfloat16)
        layer_store.append(
            (
                normed_one,
                scale_one,
                attn_in,
                query_b,
                key_win,
                value_win,
                log_total,
                attended,
                normed_two,
                scale_two,
                ffn_in,
                gate_part,
                linear_part,
                hidden_b,
            )
        )
        stream = middle + dot_cols(hidden_b, down_all[layer_index])
    back_one, back_qkv, back_out, back_two, back_up, back_down = (
        gains_one,
        qkv_all,
        out_all,
        gains_two,
        up_all,
        down_all,
    )
    grad_stream = cotangent.reshape(row_count, D)
    layer_grads = [None] * LAYERS
    for layer_index in reversed(range(LAYERS)):
        (
            normed_one,
            scale_one,
            attn_in,
            query_b,
            key_win,
            value_win,
            log_total,
            attended,
            normed_two,
            scale_two,
            ffn_in,
            gate_part,
            linear_part,
            hidden_b,
        ) = layer_store[layer_index]
        grad_b = grad_stream.astype(jnp.bfloat16)
        grad_hidden = jnp.dot(grad_b, back_down[layer_index], preferred_element_type=jnp.float32)
        grad_lifted = jnp.concatenate(
            [
                grad_hidden * linear_part * gelu_slope(gate_part),
                grad_hidden * gelu_value(gate_part),
            ],
            axis=1,
        ).astype(jnp.bfloat16)
        grad_ffn_in = dot_cols(grad_lifted, back_up[layer_index])
        gain_two_vec = jnp.sum(grad_ffn_in * normed_two, axis=0)
        grad_middle = grad_stream + norm_back(
            grad_ffn_in, normed_two, scale_two, back_two[layer_index]
        )
        grad_middle_b = grad_middle.astype(jnp.bfloat16)
        grad_attended = (
            dot_cols(grad_middle_b, back_out[layer_index])
            .astype(jnp.bfloat16)
            .reshape(1, row_count, H, HD)
        )
        grad_query, grad_key_win, grad_value_win = attend_backward(
            query_b, key_win, value_win, window_mask, log_total, grad_attended, score_scale
        )
        window_grads = jnp.concatenate(
            [grad_key_win.reshape(1, width_keys, D), grad_value_win.reshape(1, width_keys, D)],
            axis=2,
        )
        edge_grads = jnp.concatenate(
            [window_grads[:, :HALF], window_grads[:, HALF + row_count :]], axis=1
        )
        returned = with_halo(edge_grads.astype(jnp.bfloat16), (("seq", 1),), HALF).astype(
            edge_grads.dtype
        )
        filler = jnp.zeros((1, row_count - 2 * HALF, 2 * D), jnp.float32)
        own_grads = window_grads[:, HALF : HALF + row_count] + jnp.concatenate(
            [returned[:, :HALF], filler, returned[:, 3 * HALF :]], axis=1
        )
        own_grads = own_grads.reshape(row_count, 2 * D)
        grad_query = grad_query.reshape(row_count, H, HD)
        grad_key = own_grads[:, :D].reshape(row_count, H, HD)
        grad_query_pre = grad_query * cosine_table + rotate_back(grad_query * sine_table)
        grad_key_pre = grad_key * cosine_table + rotate_back(grad_key * sine_table)
        grad_projected = jnp.concatenate(
            [
                grad_query_pre.reshape(row_count, D),
                grad_key_pre.reshape(row_count, D),
                own_grads[:, D:],
            ],
            axis=1,
        ).astype(jnp.bfloat16)
        grad_attn_in = dot_cols(grad_projected, back_qkv[layer_index])
        gain_one_vec = jnp.sum(grad_attn_in * normed_one, axis=0)
        grad_stream = grad_middle + norm_back(
            grad_attn_in, normed_one, scale_one, back_one[layer_index]
        )
        layer_grads[layer_index] = scatter_layer(
            (
                dot_rows(attn_in, grad_projected),
                dot_rows(attended, grad_middle_b),
                dot_rows(ffn_in, grad_lifted),
                dot_rows(grad_b, hidden_b),
            ),
            (gain_one_vec, gain_two_vec),
            grad_factor,
        )
    qkv_part, out_part, up_part, down_part, gain_one_part, gain_two_part = map(
        jnp.stack, zip(*layer_grads)
    )
    return (
        stream.reshape(1, row_count, D),
        grad_stream.reshape(1, row_count, D),
        qkv_part,
        out_part,
        up_part,
        down_part,
        gain_one_part,
        gain_two_part,
    )


def solution(mesh):
    placed = (
        P("fsdp", "seq", None),
        P("fsdp", "seq", None),
        P(None, ("seq", "fsdp"), None),
        P(None, ("seq", "fsdp"), None),
        P(None, ("seq", "fsdp"), None),
        P(None, ("seq", "fsdp"), None),
        P(None, ("seq", "fsdp")),
        P(None, ("seq", "fsdp")),
    )
    return jax.shard_map(
        local,
        mesh=mesh,
        in_specs=placed,
        out_specs=(
            P("fsdp", "seq", None),
            P("fsdp", "seq", None),
            P(None, ("seq", "fsdp"), None),
            P(None, ("seq", "fsdp"), None),
            P(None, ("seq", "fsdp"), None),
            P(None, ("seq", "fsdp"), None),
            P(None, ("seq", "fsdp")),
            P(None, ("seq", "fsdp")),
        ),
        check_vma=False,
    )
```

```python
import functools
import math

import jax
import jax.numpy as jnp
from jax import lax
from jax.experimental import pallas as pl
from jax.experimental.pallas import tpu as pltpu
from jax.sharding import PartitionSpec as P


D = 768
H = 12
HD = 64
FF = 1152
HALF = 64
LAYERS = 2
LANES = 128


norm_eps = 1e-05
rope_base = 10000.0
inv_root_two = 1.0 / math.sqrt(2.0)
inv_root_tau = 1.0 / math.sqrt(2.0 * math.pi)
score_scale = 1.0 / math.sqrt(HD)
bf16 = jnp.bfloat16
f32 = jnp.float32


def rope_tables(positions, head_size):
    frequency = rope_base ** (-jnp.arange(0, head_size, 2).astype(f32) / head_size)
    angles = positions[:, None] * frequency[None, :]
    cosine = jnp.cos(angles)
    sine_part = jnp.sin(angles)
    return jnp.tile(cosine, (1, 2 * H)), jnp.tile(sine_part, (1, 2 * H))


def dot_plain(left_side, right_side):
    return jnp.dot(left_side, right_side, preferred_element_type=f32)


def dot_rows(left_side, right_side):
    return lax.dot_general(
        left_side, right_side, (((0,), (0,)), ((), ())), preferred_element_type=f32
    )


def dot_cols(left_side, right_side):
    return lax.dot_general(
        left_side, right_side, (((1,), (1,)), ((), ())), preferred_element_type=f32
    )


def layer_norm(values, norm_gain):
    center = values - jnp.mean(values, axis=-1, keepdims=True)
    inv_scale = lax.rsqrt(jnp.mean(center * center, axis=-1, keepdims=True) + norm_eps)
    normed = center * inv_scale
    return (normed, inv_scale, normed * norm_gain)


def norm_back(grad_out, normed, inv_scale, norm_gain):
    grad_hat = grad_out * norm_gain
    mean_one = jnp.mean(grad_hat, axis=-1, keepdims=True)
    mean_two = jnp.mean(grad_hat * normed, axis=-1, keepdims=True)
    return inv_scale * (grad_hat - mean_one - normed * mean_two)


def half_rolls(values):
    width = values.shape[1]
    lane = lax.broadcasted_iota(jnp.int32, values.shape, 1) % HD
    ahead = pltpu.roll(values, width - HD // 2, 1)
    behind = pltpu.roll(values, HD // 2, 1)
    return lane < HD // 2, ahead, behind


def rotate(values, cosine, sine):
    low, ahead, behind = half_rolls(values)
    return values * cosine + jnp.where(low, -ahead, behind) * sine


def rotate_back(values, cosine, sine):
    low, ahead, behind = half_rolls(values * sine)
    return values * cosine + jnp.where(low, ahead, -behind)


def window_mask(first_row, row_count, length):
    shape = (row_count, row_count + 2 * HALF)
    key = lax.broadcasted_iota(jnp.int32, shape, 1)
    offset = key - lax.broadcasted_iota(jnp.int32, shape, 0)
    place = key + (first_row - HALF)
    return (offset >= 0) & (offset <= 2 * HALF) & (place >= 0) & (place < length)


def fill_window(window_ref, own_ref, before_ref, after_ref):
    rows = own_ref.shape[0]
    window_ref[:HALF] = before_ref[...]
    window_ref[HALF : HALF + rows] = own_ref[...]
    window_ref[HALF + rows :] = after_ref[...]


def pair_cols(ref, pair, base=0):
    return ref[:, base + pair * LANES : base + (pair + 1) * LANES]


def of_head(values, side):
    lane = lax.broadcasted_iota(jnp.int32, values.shape, 1)
    return jnp.where(lane // HD == side, values, jnp.zeros_like(values))


def project_kernel(stream_ref, gain_ref, weight_ref, cos_ref, sin_ref, *outs):
    normed_ref, scale_ref, input_ref, query_ref, keyval_ref = outs
    normed, scale, pre = layer_norm(stream_ref[...], gain_ref[...])
    attn_in = pre.astype(bf16)
    normed_ref[...] = normed
    scale_ref[...] = scale
    input_ref[...] = attn_in
    cosine, sine = cos_ref[...], sin_ref[...]
    query_ref[...] = rotate(dot_plain(attn_in, weight_ref[:, :D]), cosine, sine).astype(bf16)
    keys = dot_plain(attn_in, weight_ref[:, D : 2 * D])
    keyval_ref[:, :D] = rotate(keys, cosine, sine).astype(bf16)
    keyval_ref[:, D:] = dot_plain(attn_in, weight_ref[:, 2 * D :]).astype(bf16)


def forward_kernel(length, place_ref, query_ref, keyval_ref, before_ref, after_ref, stream_ref,
                   gain_ref, out_ref, up_ref, down_ref, *rest):
    attended_ref, total_ref, normed_ref, scale_ref, input_ref = rest[:5]
    gate_ref, linear_ref, hidden_ref, result_ref, window_ref = rest[5:]
    rows = query_ref.shape[0]
    fill_window(window_ref, keyval_ref, before_ref, after_ref)
    mask = window_mask(place_ref[0], rows, length)
    lane = lax.broadcasted_iota(jnp.int32, (rows, LANES), 1)
    totals = jnp.zeros((rows, LANES), f32)
    for pair in range(H // 2):
        query = pair_cols(query_ref, pair)
        keys = pair_cols(window_ref, pair)
        values = pair_cols(window_ref, pair, D)
        mixed = []
        for side in range(2):
            scores = dot_cols(of_head(query, side), keys) * score_scale
            scores = jnp.where(mask, scores, -jnp.inf)
            log_total = jnp.log(jnp.sum(jnp.exp(scores), axis=-1, keepdims=True))
            probs = jnp.exp(scores - log_total).astype(bf16)
            mixed.append(dot_plain(probs, values))
            totals = jnp.where(lane == 2 * pair + side, log_total, totals)
        attended_ref[:, pair * LANES : (pair + 1) * LANES] = jnp.where(
            lane // HD == 0, mixed[0], mixed[1]
        ).astype(bf16)
    total_ref[...] = totals
    middle = stream_ref[...] + dot_plain(attended_ref[...], out_ref[...])
    normed, scale, pre = layer_norm(middle, gain_ref[...])
    ffn_in = pre.astype(bf16)
    normed_ref[...] = normed
    scale_ref[...] = scale
    input_ref[...] = ffn_in
    gate = dot_plain(ffn_in, up_ref[:, :FF])
    linear = dot_plain(ffn_in, up_ref[:, FF:])
    gate_ref[...] = gate
    linear_ref[...] = linear
    hidden = (0.5 * gate * (1.0 + lax.erf(gate * inv_root_two)) * linear).astype(bf16)
    hidden_ref[...] = hidden
    result_ref[...] = middle + dot_cols(hidden, down_ref[...])


def backward_kernel(length, place_ref, grad_ref, normed_ref, scale_ref, gate_ref, linear_ref,
                    gain_ref, down_ref, up_ref, out_ref, query_ref, keyval_ref, before_ref,
                    after_ref, total_ref, cos_ref, sin_ref, *rest):
    rounded_ref, lifted_ref, middle_ref, middle_b_ref, gain_sum_ref = rest[:5]
    grad_query_ref, own_ref, to_before_ref, to_after_ref, window_ref, queries_ref = rest[5:]
    rows = query_ref.shape[0]
    grad = grad_ref[...]
    grad_b = grad.astype(bf16)
    rounded_ref[...] = grad_b
    grad_hidden = dot_plain(grad_b, down_ref[...])
    gate = gate_ref[...]
    curve = 0.5 * (1.0 + lax.erf(gate * inv_root_two))
    slope = curve + gate * inv_root_tau * jnp.exp(-0.5 * gate * gate)
    lifted_ref[:, :FF] = (grad_hidden * linear_ref[...] * slope).astype(bf16)
    lifted_ref[:, FF:] = (grad_hidden * (gate * curve)).astype(bf16)
    grad_in = dot_cols(lifted_ref[...], up_ref[...])
    normed = normed_ref[...]
    gain_sum_ref[...] = jnp.sum(grad_in * normed, axis=0, keepdims=True)
    grad_middle = grad + norm_back(grad_in, normed, scale_ref[...], gain_ref[...])
    middle_ref[...] = grad_middle
    grad_middle_b = grad_middle.astype(bf16)
    middle_b_ref[...] = grad_middle_b
    grad_attended = dot_cols(grad_middle_b, out_ref[...]).astype(bf16)
    fill_window(window_ref, keyval_ref, before_ref, after_ref)
    mask = window_mask(place_ref[0], rows, length)
    lane = lax.broadcasted_iota(jnp.int32, (rows, LANES), 1)
    for pair in range(H // 2):
        query = pair_cols(query_ref, pair)
        keys = pair_cols(window_ref, pair)
        values = pair_cols(window_ref, pair, D)
        grads = grad_attended[:, pair * LANES : (pair + 1) * LANES]
        grad_query = []
        grad_keys = jnp.zeros((rows + 2 * HALF, LANES), f32)
        grad_values = jnp.zeros((rows + 2 * HALF, LANES), f32)
        for side in range(2):
            head_query = of_head(query, side)
            head_grads = of_head(grads, side)
            scores = dot_cols(head_query, keys) * score_scale
            scores = jnp.where(mask, scores, -jnp.inf)
            head = 2 * pair + side
            probs = jnp.exp(scores - total_ref[:, head : head + 1])
            grad_values = grad_values + dot_rows(probs.astype(bf16), head_grads)
            grad_probs = dot_cols(head_grads, values)
            row_inner = jnp.sum(probs * grad_probs, axis=-1, keepdims=True)
            grad_scores = (probs * (grad_probs - row_inner) * score_scale).astype(bf16)
            grad_query.append(dot_plain(grad_scores, keys))
            grad_keys = grad_keys + dot_rows(grad_scores, head_query)
        cols = slice(pair * LANES, (pair + 1) * LANES)
        queries_ref[:, cols] = jnp.where(lane // HD == 0, grad_query[0], grad_query[1])
        for base, part in ((0, grad_keys), (D, grad_values)):
            cols = slice(base + pair * LANES, base + (pair + 1) * LANES)
            to_before_ref[:, cols] = part[:HALF].astype(bf16)
            own_ref[:, cols] = part[HALF : HALF + rows]
            to_after_ref[:, cols] = part[HALF + rows :].astype(bf16)
    grad_query_ref[...] = rotate_back(queries_ref[...], cos_ref[...], sin_ref[...]).astype(bf16)


def input_grad_kernel(grad_query_ref, own_ref, before_ref, after_ref, weight_ref, gain_ref,
                      normed_ref, scale_ref, middle_ref, cos_ref, sin_ref, *outs):
    projected_ref, result_ref, gain_sum_ref, total_ref = outs
    rows = own_ref.shape[0]
    total_ref[...] = own_ref[...]
    total_ref[:HALF] = total_ref[:HALF] + before_ref[...].astype(f32)
    total_ref[rows - HALF :] = total_ref[rows - HALF :] + after_ref[...].astype(f32)
    projected_ref[:, :D] = grad_query_ref[...]
    keys = rotate_back(total_ref[:, :D], cos_ref[...], sin_ref[...])
    projected_ref[:, D : 2 * D] = keys.astype(bf16)
    projected_ref[:, 2 * D :] = total_ref[:, D:].astype(bf16)
    grad_in = dot_cols(projected_ref[...], weight_ref[...])
    normed = normed_ref[...]
    gain_sum_ref[...] = jnp.sum(grad_in * normed, axis=0, keepdims=True)
    result_ref[...] = middle_ref[...] + norm_back(
        grad_in, normed, scale_ref[...], gain_ref[...]
    )


def weight_grad_kernel(core_count, pairs, vectors, place_ref, *refs):
    sides, vector_refs, outs = (
        refs[: 2 * pairs], refs[2 * pairs : 2 * pairs + vectors], refs[2 * pairs + vectors : -2]
    )
    flipped_ref, picked_ref = refs[-2:]
    groups, rows = flipped_ref.shape[0] // core_count, flipped_ref.shape[1]
    jobs = [(sides[2 * at][...], sides[2 * at + 1]) for at in range(pairs)]
    if vectors:
        shape = (LANES, vector_refs[0].shape[1])
        row = lax.broadcasted_iota(jnp.int32, shape, 0)
        stacked = jnp.zeros(shape, f32)
        for at, vector_ref in enumerate(vector_refs):
            stacked = jnp.where(row == at, vector_ref[...], stacked)
        jobs.append((stacked.astype(bf16), None))
    first = 0
    for left, right_ref in jobs:
        flipped_ref[...] = left.T.reshape(flipped_ref.shape)
        width = LANES if right_ref is None else right_ref.shape[1]
        for shift in range(core_count):
            core = lax.rem(place_ref[0] + shift, core_count)
            for group in range(groups):
                picked_ref[group * rows : (group + 1) * rows] = flipped_ref[
                    group * core_count + core
                ]
            part = picked_ref[...]
            if right_ref is not None:
                part = dot_plain(part, right_ref[...]).astype(bf16)
            target = outs[0] if shift == 0 else outs[shift]
            target[:, first : first + width] = part
        first += width


def columns(array, first, width):
    return (array, slice(first, first + width))


def call(kernel, outs, args, scratch=(), scalar=None, flops=0):
    arrays, views = [], []
    for arg in args:
        array, cols = arg if isinstance(arg, tuple) else (arg, None)
        spot = next((k for k, held in enumerate(arrays) if held is array), len(arrays))
        if spot == len(arrays):
            arrays.append(array)
        views.append((spot, cols))
    lead, count = 0 if scalar is None else 1, len(arrays)

    def body(*refs):
        given = refs[lead : lead + count]
        seen = [given[k] if cols is None else given[k].at[:, cols] for k, cols in views]
        kernel(*refs[:lead], *seen, *refs[lead + count :])

    specs = [pl.BlockSpec(memory_space=pltpu.VMEM)] * len(arrays)
    if scalar is not None:
        specs = [pl.BlockSpec(memory_space=pltpu.SMEM), *specs]
        arrays = [scalar, *arrays]
    moved = sum(math.prod(shape) * jnp.dtype(kind).itemsize for shape, kind in outs)
    moved += sum(a.size * a.dtype.itemsize for a in arrays[lead:])

    def run(*operands):
        return pl.pallas_call(
            body,
            out_shape=[jax.ShapeDtypeStruct(shape, kind) for shape, kind in outs],
            in_specs=specs,
            out_specs=[pl.BlockSpec(memory_space=pltpu.VMEM)] * len(outs),
            scratch_shapes=[pltpu.VMEM(shape, kind) for shape, kind in scratch],
            cost_estimate=pl.CostEstimate(flops=flops, bytes_accessed=moved, transcendentals=0),
            compiler_params=pltpu.CompilerParams(vmem_limit_bytes=24 << 20),
        )(*operands)

    return run(*arrays)


def place_kernel(own_ref, held_ref, arrived_ref, out_ref):
    own = own_ref[0]
    out_ref[0, pl.ds(own, 1)] = held_ref[...]
    out_ref[0, pl.ds(1 - own, 1)] = arrived_ref[...]


def place_pair(held, arrived, dim, own):
    outer, width = math.prod(held.shape[:dim]), held.shape[-1]
    rows = math.prod(held.shape[dim:-1])
    block = pl.BlockSpec((1, rows, width), lambda i: (i, 0, 0))
    placed = pl.pallas_call(
        place_kernel,
        grid=(outer,),
        out_shape=jax.ShapeDtypeStruct((outer, 2, rows, width), held.dtype),
        in_specs=[pl.BlockSpec(memory_space=pltpu.SMEM), block, block],
        out_specs=pl.BlockSpec((1, 2, rows, width), lambda i: (i, 0, 0, 0)),
        cost_estimate=pl.CostEstimate(
            flops=0, bytes_accessed=4 * held.size * held.dtype.itemsize, transcendentals=0
        ),
        compiler_params=pltpu.CompilerParams(vmem_limit_bytes=12 << 20),
    )(own.astype(jnp.int32).reshape(1), *(
        cells.reshape(outer, rows, width) for cells in (held, arrived)
    ))
    return placed.reshape(*held.shape[:dim], 2, *held.shape[dim:])


def digits_of(seq_count, shard_count):
    core_count = 2 if seq_count % 2 == 0 else 1
    left = seq_count // core_count
    sizes = []
    while left > 1:
        size = 4 if left % 4 == 0 else 2 if left % 2 == 0 else left
        sizes.append(size)
        left //= size
    digits = []
    stride = seq_count
    for size in (*sizes, core_count):
        stride //= size
        digits.append(("seq", stride, size))
    return (*digits, ("fsdp", 1, shard_count))


def digit_orders(digits):
    core = len(digits) - 2
    near = [core + 1, *reversed(range(core))]
    return (near, [*near[1:2], near[0], *near[2:]])


def own_digit(digit):
    axis, stride, size = digit
    return (lax.axis_index(axis) // stride) % size


def partner(held, shift, size):
    return held ^ shift if size & (size - 1) == 0 else (held + shift) % size


def shift_between(own, place, size):
    return own ^ place if size & (size - 1) == 0 else (own - place) % size


def shift_digit(cells, digit, shift):
    axis, stride, size = digit
    pairs = []
    for index in range(lax.axis_size(axis)):
        held = (index // stride) % size
        pairs.append((index, index + (partner(held, shift, size) - held) * stride))
    return lax.ppermute(cells, axis, pairs)


def take_block(cells, dim, index):
    return lax.dynamic_index_in_dim(cells, index, axis=dim, keepdims=False)


def added(parts):
    total = parts[0].astype(f32)
    for part in parts[1:]:
        total = total + part.astype(f32)
    return total


def blocks_to_send(parts, dim, digit):
    own, size = own_digit(digit), digit[2]
    return [
        added([take_block(part, dim, partner(own, shift, size)) for part in parts]).astype(bf16)
        for shift in range(1, size)
    ]


def sum_digit(parts, blocks, dim, digit):
    own = own_digit(digit)
    arrived = [shift_digit(cells, digit, at + 1) for at, cells in enumerate(blocks)]
    return added([take_block(part, dim, own) for part in parts] + arrived)


def gather_digit(cells, dim, digit):
    size = digit[2]
    own = own_digit(digit)
    arrived = [cells] + [shift_digit(cells, digit, shift) for shift in range(1, size)]
    if size == 2:
        return place_pair(cells, arrived[1], dim, own)
    placed = []
    for place in range(size):
        block = arrived[0]
        for shift in range(1, size):
            block = jnp.where(shift_between(own, place, size) == shift, arrived[shift], block)
        placed.append(block)
    return jnp.stack(placed, axis=dim)


def gather_order(digits, color):
    return [*reversed(digit_orders(digits)[color]), len(digits) - 2]


def gather_rows(shard, color):
    digits = digits_of(lax.axis_size("seq"), lax.axis_size("fsdp"))
    held = []
    for index in gather_order(digits, color):
        dim = sum(other < index for other in held)
        shard = gather_digit(shard, dim, digits[index])
        held.append(index)
    return shard.reshape(-1, shard.shape[-1])


def sum_order(digits, color):
    return [len(digits) - 2, *digit_orders(digits)[color]]


def sum_begin(sent, kept, color):
    digits = digits_of(lax.axis_size("seq"), lax.axis_size("fsdp"))
    core, *near = sum_order(digits, color)
    sizes = [digit[2] for digit in digits]
    parts = [kept] + [
        shift_digit(sent[shift - 1], digits[core], shift)
        for shift in range(1, sizes[core])
    ]
    parts = [part.reshape(*sizes[:core], sizes[-1], -1, part.shape[-1]) for part in parts]
    held = [index for index in range(len(digits)) if index != core]
    return parts, blocks_to_send(parts, held.index(near[0]), digits[near[0]])


def sum_end(parts, blocks, color):
    digits = digits_of(lax.axis_size("seq"), lax.axis_size("fsdp"))
    core, *near = sum_order(digits, color)
    held = [index for index in range(len(digits)) if index != core]
    for stage, index in enumerate(near):
        dim = held.index(index)
        if stage:
            blocks = blocks_to_send(parts, dim, digits[index])
        total = sum_digit(parts, blocks, dim, digits[index])
        parts = [total.astype(bf16)]
        held.remove(index)
    return total


def local(tokens, cotangent, qkv_weight, out_weight, up_weight, down_weight, attn_gain, mlp_gain):
    row_count = tokens.shape[1]
    seq_count = lax.axis_size("seq")
    shard_count = lax.axis_size("fsdp")
    first_row = lax.axis_index("seq") * row_count
    length = row_count * seq_count
    digits = digits_of(seq_count, shard_count)
    core_count = digits[-2][2]
    own_core = own_digit(digits[-2]).astype(jnp.int32).reshape(1)
    place = first_row.astype(jnp.int32).reshape(1)
    grad_factor = 1.0 / math.sqrt(length * shard_count)
    positions = (first_row + jnp.arange(row_count)).astype(f32)
    cosine, sine = rope_tables(positions, HD)
    ends = seq_count - 1
    onward = [(i, i + 1) for i in range(ends)]
    back = [(i + 1, i) for i in range(ends)]

    def halo(cells, pairs):
        return lax.ppermute(cells, "seq", pairs)

    stream = tokens.reshape(row_count, D)
    gains = jnp.concatenate([attn_gain, mlp_gain]).T
    gains = jnp.pad(gains, ((0, 0), (0, LANES - 2 * LAYERS)))
    mixing, widening = [], []
    for n in range(LAYERS):
        packed = [qkv_weight[n], out_weight[n]] + ([gains] if n == 0 else [])
        mixing.append(gather_rows(jnp.concatenate(packed, axis=1), 0))
        packed = jnp.concatenate([up_weight[n], down_weight[n]], axis=1)
        widening.append(gather_rows(packed, 1))
    gains = mixing[0][:, 4 * D : 4 * D + 2 * LAYERS].T
    qkv_all = [columns(array, 0, 3 * D) for array in mixing]
    out_all = [columns(array, 3 * D, D) for array in mixing]
    up_all = [columns(array, 0, 2 * FF) for array in widening]
    down_all = [columns(array, 2 * FF, FF) for array in widening]
    gains_one, gains_two = gains[:LAYERS, None].astype(f32), gains[LAYERS:, None].astype(f32)
    wide = ((row_count, D), f32)
    wide_b = ((row_count, D), bf16)
    column = ((row_count, 1), f32)
    vector = ((1, D), f32)
    edge = ((HALF, 2 * D), bf16)
    lifted_f = ((row_count, FF), f32)
    window = ((row_count + 2 * HALF, 2 * D), bf16)
    unit = 2 * row_count * D
    layer_store = []
    for n in range(LAYERS):
        normed_one, scale_one, attn_in, query, keyval = call(
            project_kernel,
            [wide, column, wide_b, wide_b, ((row_count, 2 * D), bf16)],
            (stream, gains_one[n], qkv_all[n], cosine, sine),
            flops=unit * 3 * D,
        )
        before = halo(keyval[row_count - HALF :], onward)
        after = halo(keyval[:HALF], back)
        (attended, totals, normed_two, scale_two, ffn_in, gate, linear, hidden, stream) = call(
            functools.partial(forward_kernel, length),
            [wide_b, ((row_count, LANES), f32), wide, column, wide_b, lifted_f, lifted_f,
             ((row_count, FF), bf16), wide],
            (query, keyval, before, after, stream, gains_two[n], out_all[n], up_all[n],
             down_all[n]),
            scratch=[window],
            scalar=place,
            flops=unit * (D + 3 * FF),
        )
        layer_store.append(
            (normed_one, scale_one, attn_in, query, keyval, before, after, attended, totals,
             normed_two, scale_two, ffn_in, gate, linear, hidden)
        )
    grad_stream = cotangent.reshape(row_count, D)
    layer_grads = [None] * LAYERS
    sums = []
    chips = D // (seq_count * shard_count) * shard_count

    def weight_grads(sides, vectors=()):
        width = sum(side[1].shape[1] for side in sides) + (LANES if vectors else 0)
        half_rows = D // core_count
        outs = call(
            functools.partial(weight_grad_kernel, core_count, len(sides), len(vectors)),
            [((half_rows, width), bf16)] * core_count,
            [array for side in sides for array in side] + list(vectors),
            scratch=[((D // chips, chips, row_count), bf16), ((half_rows, row_count), bf16)],
            scalar=own_core,
            flops=unit * width,
        )
        return outs[1:], outs[0]

    for n in reversed(range(LAYERS)):
        (normed_one, scale_one, attn_in, query, keyval, before, after, attended, totals,
         normed_two, scale_two, ffn_in, gate, linear, hidden) = layer_store[n]
        (grad_b, grad_lifted, grad_middle, grad_middle_b, gain_two_vec, grad_query, own_grads,
         to_before, to_after) = call(
            functools.partial(backward_kernel, length),
            [wide_b, ((row_count, 2 * FF), bf16), wide, wide_b, vector, wide_b,
             ((row_count, 2 * D), f32), edge, edge],
            (grad_stream, normed_two, scale_two, gate, linear, gains_two[n], down_all[n],
             up_all[n], out_all[n], query, keyval, before, after, totals, cosine, sine),
            scratch=[window, wide],
            scalar=place,
            flops=unit * (D + 3 * FF),
        )
        from_before = halo(to_after, onward)
        from_after = halo(to_before, back)
        outer = weight_grads([(ffn_in, grad_lifted), (grad_b, hidden)])
        grad_projected, grad_stream, gain_one_vec = call(
            input_grad_kernel,
            [((row_count, 3 * D), bf16), wide, vector],
            (grad_query, own_grads, from_before, from_after, qkv_all[n], gains_one[n],
             normed_one, scale_one, grad_middle, cosine, sine),
            scratch=[((row_count, 2 * D), f32)],
            flops=unit * 3 * D,
        )
        inner = weight_grads(
            [(attn_in, grad_projected), (attended, grad_middle_b)], (gain_one_vec, gain_two_vec)
        )
        outer = sum_begin(*outer, 1)
        inner = sum_begin(*inner, 0)
        if n:
            grad_stream, outer, inner = lax.optimization_barrier((grad_stream, outer, inner))
        sums.append((n, outer, inner))
    for n, outer, inner in sums:
        outer = sum_end(*outer, 1)
        inner = sum_end(*inner, 0)
        layer_grads[n] = (
            inner[:, : 3 * D], inner[:, 3 * D : 4 * D], outer[:, : 2 * FF], outer[:, 2 * FF :],
            inner[:, 4 * D], inner[:, 4 * D + 1],
        )
    qkv_part, out_part, up_part, down_part, gain_one_part, gain_two_part = (
        jnp.stack(parts) * grad_factor for parts in zip(*layer_grads)
    )
    return (
        stream.reshape(1, row_count, D),
        grad_stream.reshape(1, row_count, D),
        qkv_part,
        out_part,
        up_part,
        down_part,
        gain_one_part,
        gain_two_part,
    )


def solution(mesh):
    placed = (
        P("fsdp", "seq", None),
        P("fsdp", "seq", None),
        P(None, ("seq", "fsdp"), None),
        P(None, ("seq", "fsdp"), None),
        P(None, ("seq", "fsdp"), None),
        P(None, ("seq", "fsdp"), None),
        P(None, ("seq", "fsdp")),
        P(None, ("seq", "fsdp")),
    )
    return jax.shard_map(
        local,
        mesh=mesh,
        in_specs=placed,
        out_specs=(
            P("fsdp", "seq", None),
            P("fsdp", "seq", None),
            P(None, ("seq", "fsdp"), None),
            P(None, ("seq", "fsdp"), None),
            P(None, ("seq", "fsdp"), None),
            P(None, ("seq", "fsdp"), None),
            P(None, ("seq", "fsdp")),
            P(None, ("seq", "fsdp")),
        ),
        check_vma=False,
    )
```
